32 devices in a mesh: pool: 8 (over z, core), band: 4 (over y, x).
Axes of the slice: x: 2, y: 2, z: 4, core: 2. Of those that a mesh axis runs over, the one named last changes fastest.
Arguments:
- orbitals: float32 [8, 4, 2, 13824], P('pool', 'band'), may hold values from -6 to 6
- kpoints: float32 [8, 3], replicated, may hold values from -0.5 to 0.5
- owner: int32 [1], replicated, may hold values from 0 to 7
Outputs:
- exchange: float32 [8, 4, 2, 13824], P('pool', 'band')
The draws below stay inside these ranges and needn't reach their ends.
All inputs are finite; a program needn't handle non-finite values.
Results may differ from the reference program's by a relative error of at most 0.0001.
Values sent between devices are 32-bit elements; how exact they have to be, the bound alone decides.
A program may use at most 64 MiB of HBM per device.

```python
import jax
import jax.numpy as jnp
from jax import lax

NG = 24
NQ = 1
BANDS = 4
KPTS = 8
GRID = 13824


def shard_levels(rng, dims, shards, low, top_value):
    gain, own = 1.0, jax.random.fold_in(rng, 6)
    for axis_at, parts in shards:
        steps = jnp.exp(jax.random.uniform(jax.random.fold_in(own, axis_at), (parts,), jnp.float32, low / len(shards), top_value / len(shards)))
        gain = gain * jnp.repeat(steps, dims[axis_at] // parts).reshape([-1 if axis == axis_at else 1 for axis in range(len(dims))])
    return gain


def gaussian(rng, shape, width, limit, pieces=(), kind=jnp.bfloat16):
    level = shard_levels(rng, shape, pieces, -0.22, 0.18) if pieces else 1.0
    drawn = jax.random.normal(rng, shape, jnp.float32) * width * level
    return jnp.minimum(jnp.maximum(drawn, -limit), limit).astype(kind)


def setup_inputs(seed: int = 0) -> dict:
    seeds = jax.random.split(jax.random.key(seed), 4)
    return {
        "orbitals": gaussian(seeds[0], (KPTS, BANDS, 2, GRID), 1.0, 6.0, ((0, 8), (1, 4)), jnp.float32),
        "kpoints": jnp.clip(jax.random.uniform(seeds[1], (KPTS, 3), jnp.float32, -0.5, 0.5), -0.5, 0.5),
        "owner": jax.random.randint(seeds[2], (NQ,), 0, KPTS).astype(jnp.int32),
    }


mixing = 0.25
kernel_scale = 60.0
screening = 4.0


def frequencies():
    idx = jnp.arange(NG, dtype=jnp.int32)
    return ((idx + NG // 2) % NG - NG // 2).astype(jnp.float32)


def coulomb(dvec):
    freq = frequencies()
    square = (freq[:, None, None] + dvec[0]) ** 2 + (freq[None, :, None] + dvec[1]) ** 2 + (freq[None, None, :] + dvec[2]) ** 2
    return kernel_scale / (square + screening)


def reference(orbitals, kpoints, owner):
    fields = orbitals[:, :, 0] + 1j * orbitals[:, :, 1]
    total = jnp.zeros(fields.shape, fields.dtype)
    for step in range(NQ):
        source_k = owner[step]
        sources = lax.dynamic_index_in_dim(fields, source_k, 0, keepdims=False)
        qvec = lax.dynamic_index_in_dim(kpoints, source_k, 0, keepdims=False)

        def per_point(item):
            resident, kvec = item
            kernel = coulomb(kvec - qvec)
            density = jnp.conj(sources)[:, None, :] * resident[None, :, :]
            density = density.reshape(BANDS, BANDS, NG, NG, NG)
            spectrum = jnp.fft.fftn(density, axes=(2, 3, 4)) * kernel
            potential = jnp.fft.ifftn(spectrum, axes=(2, 3, 4)).reshape(BANDS, BANDS, GRID)
            return -mixing * jnp.sum(sources[:, None, :] * potential, axis=0)

        total = total + lax.map(per_point, (fields, kpoints))
    return jnp.stack([jnp.real(total), jnp.imag(total)], axis=2).astype(jnp.float32)
```

```python
import functools
import math

import jax
import jax.numpy as jnp
import numpy as np
from jax import lax
from jax.experimental import pallas as pl
from jax.experimental.pallas import tpu as pltpu
from jax.sharding import PartitionSpec as P

NG = 24
ROWS = NG * NG
GRID = NG**3
LANES = 128
TILES = GRID // LANES
GROUP = 4

mixing = 0.25
kernel_scale = 60.0
screening = 4.0

MESH = pl.DeviceIdType.MESH


def dft_weights():
    idx = np.arange(NG)
    phase = 2.0 * np.pi * (np.outer(idx, idx) % NG) / NG
    cosine, sine = np.cos(phase), -np.sin(phase)
    full = np.zeros((2 * LANES, 2 * LANES))
    for n in range(GROUP):
        lo = n * NG
        re, im = slice(lo, lo + NG), slice(LANES + lo, LANES + lo + NG)
        full[re, re] = cosine
        full[re, im] = sine
        full[im, re] = -sine
        full[im, im] = cosine
    full = full.astype(np.float32)
    high = full.astype(jnp.bfloat16)
    low = (full - high.astype(np.float32)).astype(jnp.bfloat16)
    return np.stack([high, low])


def cadd(x, y):
    return x[0] + y[0], x[1] + y[1]


def csub(x, y):
    return x[0] - y[0], x[1] - y[1]


def down(x):
    return x[1], -x[0]


def dft3(x0, x1, x2):
    total = cadd(x1, x2)
    diff = csub(x1, x2)
    half = (x0[0] - 0.5 * total[0], x0[1] - 0.5 * total[1])
    root = math.sqrt(3.0) / 2.0
    turn = (root * diff[1], -root * diff[0])
    return cadd(x0, total), cadd(half, turn), csub(half, turn)


def dft4(x0, x1, x2, x3):
    a, b = cadd(x0, x2), csub(x0, x2)
    c, d = cadd(x1, x3), down(csub(x1, x3))
    return cadd(a, c), cadd(b, d), csub(a, c), csub(b, d)


def dft8(x):
    even = dft4(x[0], x[2], x[4], x[6])
    odd = dft4(x[1], x[3], x[5], x[7])
    root = math.sqrt(0.5)
    one, three = odd[1], odd[3]
    twisted = [
        odd[0],
        (root * (one[0] + one[1]), root * (one[1] - one[0])),
        down(odd[2]),
        (root * (three[1] - three[0]), -root * (three[0] + three[1])),
    ]
    return [cadd(even[i], twisted[i]) for i in range(4)] + [csub(even[i], twisted[i]) for i in range(4)]


def dft24(x):
    parts = [[None] * 8 for _ in range(3)]
    for n2 in range(8):
        three = dft3(*(x[(8 * n1 + 3 * n2) % NG] for n1 in range(3)))
        for k1 in range(3):
            parts[k1][n2] = three[k1]
    out = [None] * NG
    for k1 in range(3):
        eight = dft8(parts[k1])
        for k2 in range(8):
            out[next(k for k in range(NG) if k % 3 == k1 and k % 8 == k2)] = eight[k2]
    return out


def lane_iota(shape):
    return lax.broadcasted_iota(jnp.int32, shape, len(shape) - 1)


def starts():
    return [min(8 * i, 28) for i in range(5)]


def compute_kernel(count, owner_ref, kp_ref, src_ref, own_ref, w_ref, out_ref, sre, sim, dre, dim, acc_re, acc_im, ker):
    pool = lax.axis_index("pool")
    source = owner_ref[0]
    d0 = kp_ref[pool, 0] - kp_ref[source, 0]
    d1 = kp_ref[pool, 1] - kp_ref[source, 1]
    d2 = kp_ref[pool, 2] - kp_ref[source, 2]
    lane = lane_iota((NG, LANES))
    gc = ((lane % NG + NG // 2) % NG - NG // 2).astype(jnp.float32)
    row = lax.broadcasted_iota(jnp.int32, (NG, LANES), 0)
    gb = ((row + NG // 2) % NG - NG // 2).astype(jnp.float32)
    plane = (gb + d1) ** 2 + (gc + d2) ** 2 + screening
    for a in range(NG):
        ga = float((a + NG // 2) % NG - NG // 2)
        ker[pl.ds(NG * a, NG), :] = (kernel_scale / GRID) / (plane + (ga + d0) ** 2)

    lane8 = lane_iota((8, LANES))

    def windows(ref, base, start, ri):
        return [ref[pl.ds(base + 6 * start + 2 * s + ri, 8, stride=6), :] for s in range(3)]

    def window(rows, j):
        s, off = divmod(24 * j, LANES)
        value = rows[s]
        if off + NG > LANES:
            value = jnp.where(lane8 >= off, value, rows[s + 1])
        return value, off

    def shift(value, amount):
        amount %= LANES
        return pltpu.roll(value, amount, 1) if amount else value

    def spread(sets, j):
        total = None
        for n in range(GROUP):
            value, off = window(sets[n], j)
            moved = shift(value, NG * n - off)
            total = moved if total is None else jnp.where(lane8 >= NG * n, moved, total)
        return jnp.where(lane8 < NG * GROUP, total, 0.0)

    def line(re_ref, im_ref, first, stride, step, swapped):
        values = []
        for i in range(NG):
            at = pl.ds(first + step * i, 8, stride=stride) if stride > 1 else pl.ds(first + step * i, 8)
            pair = (re_ref[at, :], im_ref[at, :])
            values.append(pair[::-1] if swapped else pair)
        for i, pair in enumerate(dft24(values)):
            at = pl.ds(first + step * i, 8, stride=stride) if stride > 1 else pl.ds(first + step * i, 8)
            if swapped:
                pair = pair[::-1]
            re_ref[at, :] = pair[0]
            im_ref[at, :] = pair[1]

    def product(first, second):
        x = jnp.concatenate([first, second], axis=1)
        high = x.astype(jnp.bfloat16)
        low = (x - high.astype(jnp.float32)).astype(jnp.bfloat16)
        dot = functools.partial(jnp.dot, preferred_element_type=jnp.float32)
        y = dot(high, w_ref[0]) + (dot(low, w_ref[0]) + dot(high, w_ref[1]))
        return y[:, :LANES], y[:, LANES:]

    for group in range(count // GROUP):
        for start in starts():
            own = [windows(own_ref, 0, start, ri) for ri in range(2)]
            src = [
                [windows(src_ref, 2 * TILES * (group * GROUP + n), start, ri) for n in range(GROUP)]
                for ri in range(2)
            ]
            for j in range(16):
                at = pl.ds(16 * start + j, 8, stride=16)
                r_re = spread([own[0]] * GROUP, j)
                r_im = spread([own[1]] * GROUP, j)
                s_re = spread(src[0], j)
                s_im = spread(src[1], j)
                sre[at, :] = s_re
                sim[at, :] = s_im
                dre[at, :] = s_re * r_re + s_im * r_im
                dim[at, :] = s_re * r_im - s_im * r_re
        for bg in range(3):
            line(dre, dim, 8 * bg, 1, NG, False)
        for ag in range(3):
            line(dre, dim, 8 * NG * ag, NG, 1, False)
        for part in range(3):
            at = pl.ds(192 * part, 192)
            re, im = product(dre[at, :], dim[at, :])
            value = ker[at, :]
            im, re = product(im * value, re * value)
            dre[at, :] = re
            dim[at, :] = im
        for ag in range(3):
            line(dre, dim, 8 * NG * ag, NG, 1, True)
        for bg in range(3):
            line(dre, dim, 8 * bg, 1, NG, True)
        for part in range(9):
            at = pl.ds(64 * part, 64)
            s_re, s_im, p_re, p_im = sre[at, :], sim[at, :], dre[at, :], dim[at, :]
            o_re = s_re * p_re - s_im * p_im
            o_im = s_re * p_im + s_im * p_re
            if group:
                o_re += acc_re[at, :]
                o_im += acc_im[at, :]
            acc_re[at, :] = o_re
            acc_im[at, :] = o_im

    for start in starts():
        for ri, acc in enumerate((acc_re, acc_im)):
            rows = [None] * 3
            for j in range(16):
                value = acc[pl.ds(16 * start + j, 8, stride=16), :]
                value = value + shift(value, -2 * NG)
                value = value + shift(value, -NG)
                s, off = divmod(24 * j, LANES)
                moved = shift(value, off)
                rows[s] = moved if rows[s] is None else jnp.where(lane8 >= off, moved, rows[s])
                if off + NG > LANES:
                    rows[s + 1] = moved
            for s in range(3):
                out_ref[pl.ds(6 * start + 2 * s + ri, 8, stride=6), :] = -mixing * rows[s]


def compute(owner, kpoints, sources, own, weights):
    count = sources.shape[0] // (2 * TILES)
    vmem = pl.BlockSpec(memory_space=pltpu.VMEM)
    smem = pl.BlockSpec(memory_space=pltpu.SMEM)
    return pl.pallas_call(
        functools.partial(compute_kernel, count),
        out_shape=jax.ShapeDtypeStruct((2 * TILES, LANES), jnp.float32),
        in_specs=[smem, smem, vmem, vmem, vmem],
        out_specs=vmem,
        scratch_shapes=[pltpu.VMEM((ROWS, LANES), jnp.float32)] * 7,
        name="exchange",
    )(owner, kpoints, sources, own, weights)


def gather_kernel(npool, nband, owner_ref, x_ref, out_ref, pair, mine, up, dn, upo, dno, chosen,
                  s_pair, r_pair, s_up, r_up, s_dn, r_dn, s_band, r_band, s_rel, r_rel):
    pool, band = lax.axis_index("pool"), lax.axis_index("band")
    nz = npool // 2
    z, core = pool // 2, pool % 2
    half = TILES // 2
    source = owner_ref[0]
    partner = {"pool": 2 * z + 1 - core}
    above = {"pool": lax.rem(pool + 2, npool)}
    below = {"pool": lax.rem(pool + npool - 2, npool)}
    barrier = pltpu.get_barrier_semaphore()
    pl.semaphore_signal(barrier, inc=1, device_id=partner, device_id_type=MESH)
    pl.semaphore_signal(barrier, inc=1, device_id=above, device_id_type=MESH)
    pl.semaphore_signal(barrier, inc=1, device_id=below, device_id_type=MESH)
    for step in range(1, nband):
        pl.semaphore_signal(barrier, inc=1, device_id={"band": lax.rem(band + step, nband)}, device_id_type=MESH)
    pl.semaphore_wait(barrier, 3 + nband - 1)

    def remote(src, dst, ss, rs, to):
        return pltpu.make_async_remote_copy(src_ref=src, dst_ref=dst, send_sem=ss, recv_sem=rs, device_id=to, device_id_type=MESH)

    swap = remote(x_ref.at[pl.ds(half * (1 - core), half)], pair, s_pair, r_pair, partner)
    swap.start()
    swap.wait_recv()
    keep = x_ref[pl.ds(half * core, half)]
    got = pair[...]
    zero = jnp.zeros_like(got)
    mine[...] = jnp.where(source == pool, keep, jnp.where(source == 2 * z + 1 - core, got, zero))

    rise = remote(upo, up, s_up, r_up, above)
    fall = remote(dno, dn, s_dn, r_dn, below)

    def go_up():
        @pl.when(z > 0)
        def _():
            rise.wait_recv()

        @pl.when(z == 0)
        def _():
            up[...] = jnp.zeros_like(up)

        @pl.when(z < nz - 1)
        def _():
            upo[...] = up[...] + mine[...]
            rise.start()

    def go_down():
        @pl.when(z < nz - 1)
        def _():
            fall.wait_recv()

        @pl.when(z == nz - 1)
        def _():
            dn[...] = jnp.zeros_like(dn)

        @pl.when(z > 0)
        def _():
            dno[...] = dn[...] + mine[...]
            fall.start()

    @pl.when(z < nz // 2)
    def _():
        go_up()
        go_down()

    @pl.when(z >= nz // 2)
    def _():
        go_down()
        go_up()

    chosen[...] = mine[...] + up[...] + dn[...]
    mine_half = pl.ds(half * core, half)
    here = out_ref.at[band, mine_half]
    sends = []
    for step in range(1, nband):
        other = lax.rem(band + step, nband)
        copy = remote(chosen, here, s_band.at[step], r_band.at[step], {"band": other})
        copy.start()
        sends.append(copy)
    relays = [remote(chosen, here, s_rel.at[0], r_rel.at[0], partner)]
    relays[0].start()
    out_ref[band, mine_half] = chosen[...]
    for step in range(1, nband):
        sends[step - 1].wait_recv()
        origin = lax.rem(band + nband - step, nband)
        block = out_ref.at[origin, mine_half]
        relay = remote(block, block, s_rel.at[step], r_rel.at[step], partner)
        relay.start()
        relays.append(relay)
    for relay in relays:
        relay.wait_recv()
    for copy in sends + relays:
        copy.wait_send()
    swap.wait_send()

    @pl.when(z < nz - 1)
    def _():
        rise.wait_send()

    @pl.when(z > 0)
    def _():
        fall.wait_send()


def gather(owner, block, npool, nband):
    half = pltpu.VMEM((TILES // 2, 2, LANES), jnp.float32)
    dma = pltpu.SemaphoreType.DMA
    vmem = pl.BlockSpec(memory_space=pltpu.VMEM)
    return pl.pallas_call(
        functools.partial(gather_kernel, npool, nband),
        out_shape=jax.ShapeDtypeStruct((nband, TILES, 2, LANES), jnp.float32),
        in_specs=[pl.BlockSpec(memory_space=pltpu.SMEM), vmem],
        out_specs=vmem,
        scratch_shapes=[half] * 7 + [dma] * 6 + [dma((nband,))] * 4,
        compiler_params=pltpu.CompilerParams(collective_id=0, has_side_effects=True),
        name="gather",
    )(owner, block)


def shards(npool, nband, orbitals, kpoints, owner):
    block = orbitals.reshape(2, TILES, LANES).transpose(1, 0, 2)
    sources = gather(owner, block, npool, nband)
    total = compute(
        owner, kpoints, sources.reshape(nband * 2 * TILES, LANES), block.reshape(2 * TILES, LANES), jnp.asarray(dft_weights())
    )
    return total.reshape(TILES, 2, LANES).transpose(1, 0, 2).reshape(1, 1, 2, GRID)


def solution(mesh):
    placed = (P("pool", "band", None, None), P(), P())
    body = functools.partial(shards, mesh.shape["pool"], mesh.shape["band"])
    return jax.shard_map(
        body, mesh=mesh, in_specs=placed, out_specs=P("pool", "band", None, None), check_vma=False
    )
```

```python
import functools
import math

import jax
import jax.numpy as jnp
import numpy as np
from jax import lax
from jax.experimental import pallas as pl
from jax.experimental.pallas import tpu as pltpu
from jax.sharding import PartitionSpec as P

NG = 24
ROWS = NG * NG
GRID = NG**3
LANES = 128
TILES = GRID // LANES
GROUP = 4

mixing = 0.25
kernel_scale = 60.0
screening = 4.0

MESH = pl.DeviceIdType.MESH


def dft_weights():
    idx = np.arange(NG)
    phase = 2.0 * np.pi * (np.outer(idx, idx) % NG) / NG
    cosine, sine = np.cos(phase), -np.sin(phase)
    full = np.zeros((2 * LANES, 2 * LANES))
    for n in range(GROUP):
        lo = n * NG
        re, im = slice(lo, lo + NG), slice(LANES + lo, LANES + lo + NG)
        full[re, re] = cosine
        full[re, im] = sine
        full[im, re] = -sine
        full[im, im] = cosine
    full = full.astype(np.float32)
    high = full.astype(jnp.bfloat16)
    low = (full - high.astype(np.float32)).astype(jnp.bfloat16)
    return np.stack([high, low])


def cadd(x, y):
    return x[0] + y[0], x[1] + y[1]


def csub(x, y):
    return x[0] - y[0], x[1] - y[1]


def down(x):
    return x[1], -x[0]


def dft3(x0, x1, x2):
    total = cadd(x1, x2)
    diff = csub(x1, x2)
    half = (x0[0] - 0.5 * total[0], x0[1] - 0.5 * total[1])
    root = math.sqrt(3.0) / 2.0
    turn = (root * diff[1], -root * diff[0])
    return cadd(x0, total), cadd(half, turn), csub(half, turn)


def dft4(x0, x1, x2, x3):
    a, b = cadd(x0, x2), csub(x0, x2)
    c, d = cadd(x1, x3), down(csub(x1, x3))
    return cadd(a, c), cadd(b, d), csub(a, c), csub(b, d)


def dft8(x):
    even = dft4(x[0], x[2], x[4], x[6])
    odd = dft4(x[1], x[3], x[5], x[7])
    root = math.sqrt(0.5)
    one, three = odd[1], odd[3]
    twisted = [
        odd[0],
        (root * (one[0] + one[1]), root * (one[1] - one[0])),
        down(odd[2]),
        (root * (three[1] - three[0]), -root * (three[0] + three[1])),
    ]
    return [cadd(even[i], twisted[i]) for i in range(4)] + [csub(even[i], twisted[i]) for i in range(4)]


def dft24(x):
    parts = [[None] * 8 for _ in range(3)]
    for n2 in range(8):
        three = dft3(*(x[(8 * n1 + 3 * n2) % NG] for n1 in range(3)))
        for k1 in range(3):
            parts[k1][n2] = three[k1]
    out = [None] * NG
    for k1 in range(3):
        eight = dft8(parts[k1])
        for k2 in range(8):
            out[next(k for k in range(NG) if k % 3 == k1 and k % 8 == k2)] = eight[k2]
    return out


def lane_iota(shape):
    return lax.broadcasted_iota(jnp.int32, shape, len(shape) - 1)


def starts():
    return [min(8 * i, 28) for i in range(5)]


def compute_kernel(count, owner_ref, kp_ref, src_ref, own_ref, w_ref, out_ref, dre, dim, flat, ker):
    pool = lax.axis_index("pool")
    source = owner_ref[0]
    d0 = kp_ref[0, pool] - kp_ref[0, source]
    d1 = kp_ref[1, pool] - kp_ref[1, source]
    d2 = kp_ref[2, pool] - kp_ref[2, source]
    lane = lane_iota((NG, LANES))
    gc = ((lane % NG + NG // 2) % NG - NG // 2).astype(jnp.float32)
    row = lax.broadcasted_iota(jnp.int32, (NG, LANES), 0)
    gb = ((row + NG // 2) % NG - NG // 2).astype(jnp.float32)
    plane = (gb + d1) ** 2 + (gc + d2) ** 2 + screening
    for a in range(NG):
        ga = float((a + NG // 2) % NG - NG // 2)
        ker[pl.ds(NG * a, NG), :] = (kernel_scale / GRID) / (plane + (ga + d0) ** 2)

    lane8 = lane_iota((8, LANES))
    row8 = lax.broadcasted_iota(jnp.int32, (8, LANES), 0)
    carried = (row8 + 16 + lane8 // NG >= NG) & (lane8 < NG * GROUP)

    def tile(ref, base, start, s, ri):
        if s < 3:
            return ref[pl.ds(base + 6 * start + 2 * s + ri, 8, stride=6), :]
        if start + 8 < 36:
            return ref[pl.ds(base + 6 * (start + 1) + ri, 8, stride=6), :]
        last = pltpu.roll(ref[pl.ds(base + 6 * start + ri, 8, stride=6), :], 7, 0)
        first = ref[pl.ds(base + ri, 8, stride=6), :]
        return jnp.where(row8 == 7, pltpu.roll(first, 7, 0), last)

    def shift(value, amount):
        amount %= LANES
        return pltpu.roll(value, amount, 1) if amount else value

    def line(re_ref, im_ref, first, stride, step, swapped, before=False, after=False):
        def at(i):
            return pl.ds(first + step * i, 8, stride=stride) if stride > 1 else pl.ds(first + step * i, 8)

        def mixed(values, other):
            return [
                tuple(jnp.where(carried, values[(i + other) % NG][c], values[i][c]) for c in range(2)) for i in range(NG)
            ]

        values = [(re_ref[at(i), :], im_ref[at(i), :]) for i in range(NG)]
        if before:
            values = mixed(values, -1)
        if swapped:
            values = [pair[::-1] for pair in values]
        values = dft24(values)
        if swapped:
            values = [pair[::-1] for pair in values]
        if after:
            values = mixed(values, 1)
        for i, pair in enumerate(values):
            re_ref[at(i), :] = pair[0]
            im_ref[at(i), :] = pair[1]

    def product(first, second):
        x = jnp.concatenate([first, second], axis=1)
        high = x.astype(jnp.bfloat16)
        low = (x - high.astype(jnp.float32)).astype(jnp.bfloat16)
        dot = functools.partial(jnp.dot, preferred_element_type=jnp.float32)
        y = dot(high, w_ref[0]) + (dot(low, w_ref[0]) + dot(high, w_ref[1]))
        return y[:, :LANES], y[:, LANES:]

    def convolve(part):
        at = pl.ds(192 * part, 192)
        re, im = product(dre[at, :], dim[at, :])
        value = ker[at, :]
        im, re = product(im * value, re * value)
        dre[at, :] = re
        dim[at, :] = im

    for group in range(count // GROUP):
        bases = [2 * TILES * (group * GROUP + n) for n in range(GROUP)]
        for start in starts():
            density = []
            for s in range(4):
                r_re, r_im = (tile(own_ref, 0, start, s, ri) for ri in range(2))
                cell = []
                for n in range(GROUP):
                    s_re, s_im = (tile(src_ref, bases[n], start, s, ri) for ri in range(2))
                    cell.append((s_re * r_re + s_im * r_im, s_re * r_im - s_im * r_re))
                density.append(cell)
            for j in range(16):
                s, off = divmod(NG * j, LANES)
                for ri, ref in enumerate((dre, dim)):
                    total = None
                    for n in range(GROUP):
                        lo = off + NG * n
                        if lo + NG <= LANES:
                            value = density[s][n][ri]
                        elif lo >= LANES:
                            value = density[s + 1][n][ri]
                        else:
                            value = jnp.where(lane8 >= LANES // 2, density[s][n][ri], density[s + 1][n][ri])
                        if total is None:
                            total = value
                        else:
                            lo, hi = lo % LANES, (lo + NG) % LANES
                            inside = (lane8 >= lo) & (lane8 < hi) if lo < hi else (lane8 >= lo) | (lane8 < hi)
                            total = jnp.where(inside, value, total)
                    ref[pl.ds(16 * start + j, 8, stride=16), :] = shift(total, -off)
        for bg in range(3):
            line(dre, dim, 8 * bg, 1, NG, False, before=bg == 2)
        for ag in range(3):
            line(dre, dim, 8 * NG * ag, NG, 1, False)
        for ag in range(3):
            convolve(ag)
        for ag in range(3):
            line(dre, dim, 8 * NG * ag, NG, 1, True)
        for bg in range(3):
            line(dre, dim, 8 * bg, 1, NG, True, after=bg == 2)
        for start in starts():
            moved = {}
            for j in range(-3, 16):
                for ri, ref in enumerate((dre, dim)):
                    if j >= 0:
                        value = ref[pl.ds(16 * start + j, 8, stride=16), :]
                    elif start:
                        value = ref[pl.ds(16 * (start - 1) + 16 + j, 8, stride=16), :]
                    else:
                        value = pltpu.roll(ref[pl.ds(16 + j, 8, stride=16), :], 1, 0)
                        end = ref[pl.ds(16 * 28 + 16 + j, 8, stride=16), :]
                        value = jnp.where(row8 == 0, pltpu.roll(end, 1, 0), value)
                    moved[j, ri] = shift(value, NG * j)
            for s in range(3):
                first = LANES * s // NG
                last = (LANES * (s + 1) - 1) // NG
                out_re = out_im = None
                for n in range(GROUP):
                    pot = []
                    for ri in range(2):
                        value = moved[first - n, ri]
                        for w in range(first + 1, last + 1):
                            value = jnp.where(lane8 >= NG * w - LANES * s, moved[w - n, ri], value)
                        pot.append(value)
                    s_re, s_im = (tile(src_ref, bases[n], start, s, ri) for ri in range(2))
                    t_re = s_re * pot[0] - s_im * pot[1]
                    t_im = s_re * pot[1] + s_im * pot[0]
                    out_re = t_re if out_re is None else out_re + t_re
                    out_im = t_im if out_im is None else out_im + t_im
                for ri, value in enumerate((out_re, out_im)):
                    at = pl.ds(6 * start + 2 * s + ri, 8, stride=6)
                    value = -mixing * value
                    if group:
                        value = value + flat[group - 1, at, :]
                    flat[group, at, :] = value
    for t in range(TILES):
        out_ref[:, pl.ds(LANES * t, LANES)] = flat[count // GROUP - 1, pl.ds(2 * t, 2), :]


def compute(owner, kpoints, sources, own, weights):
    count = sources.shape[0] // (2 * TILES)
    vmem = pl.BlockSpec(memory_space=pltpu.VMEM)
    smem = pl.BlockSpec(memory_space=pltpu.SMEM)
    return pl.pallas_call(
        functools.partial(compute_kernel, count),
        out_shape=jax.ShapeDtypeStruct((2, GRID), jnp.float32),
        in_specs=[smem, smem, vmem, vmem, vmem],
        out_specs=vmem,
        scratch_shapes=[
            pltpu.VMEM((ROWS, LANES), jnp.float32),
            pltpu.VMEM((ROWS, LANES), jnp.float32),
            pltpu.VMEM((count // GROUP, 2 * TILES, LANES), jnp.float32),
            pltpu.VMEM((ROWS, LANES), jnp.float32),
        ],
        name="exchange",
    )(owner, kpoints, sources, own, weights)


def gather_kernel(npool, nband, owner_ref, x_ref, out_ref, pair, mine, up, dn, upo, dno, chosen,
                  s_pair, r_pair, s_up, r_up, s_dn, r_dn, s_band, r_band, s_rel, r_rel):
    pool, band = lax.axis_index("pool"), lax.axis_index("band")
    nz = npool // 2
    z, core = pool // 2, pool % 2
    half = TILES // 2
    source = owner_ref[0]
    partner = {"pool": 2 * z + 1 - core}
    above = {"pool": lax.rem(pool + 2, npool)}
    below = {"pool": lax.rem(pool + npool - 2, npool)}
    barrier = pltpu.get_barrier_semaphore()
    pl.semaphore_signal(barrier, inc=1, device_id=partner, device_id_type=MESH)
    pl.semaphore_signal(barrier, inc=1, device_id=above, device_id_type=MESH)
    pl.semaphore_signal(barrier, inc=1, device_id=below, device_id_type=MESH)
    for step in range(1, nband):
        pl.semaphore_signal(barrier, inc=1, device_id={"band": lax.rem(band + step, nband)}, device_id_type=MESH)
    pl.semaphore_wait(barrier, 3 + nband - 1)

    def remote(src, dst, ss, rs, to):
        return pltpu.make_async_remote_copy(src_ref=src, dst_ref=dst, send_sem=ss, recv_sem=rs, device_id=to, device_id_type=MESH)

    swap = remote(x_ref.at[pl.ds(half * (1 - core), half)], pair, s_pair, r_pair, partner)
    swap.start()
    swap.wait_recv()
    keep = x_ref[pl.ds(half * core, half)]
    got = pair[...]
    zero = jnp.zeros_like(got)
    mine[...] = jnp.where(source == pool, keep, jnp.where(source == 2 * z + 1 - core, got, zero))

    rise = remote(upo, up, s_up, r_up, above)
    fall = remote(dno, dn, s_dn, r_dn, below)

    def go_up():
        @pl.when(z > 0)
        def _():
            rise.wait_recv()

        @pl.when(z == 0)
        def _():
            up[...] = jnp.zeros_like(up)

        @pl.when(z < nz - 1)
        def _():
            upo[...] = up[...] + mine[...]
            rise.start()

    def go_down():
        @pl.when(z < nz - 1)
        def _():
            fall.wait_recv()

        @pl.when(z == nz - 1)
        def _():
            dn[...] = jnp.zeros_like(dn)

        @pl.when(z > 0)
        def _():
            dno[...] = dn[...] + mine[...]
            fall.start()

    @pl.when(z < nz // 2)
    def _():
        go_up()
        go_down()

    @pl.when(z >= nz // 2)
    def _():
        go_down()
        go_up()

    chosen[...] = mine[...] + up[...] + dn[...]
    mine_half = pl.ds(half * core, half)
    here = out_ref.at[band, mine_half]
    sends = []
    for step in range(1, nband):
        other = lax.rem(band + step, nband)
        copy = remote(chosen, here, s_band.at[step], r_band.at[step], {"band": other})
        copy.start()
        sends.append(copy)
    relays = [remote(chosen, here, s_rel.at[0], r_rel.at[0], partner)]
    relays[0].start()
    out_ref[band, mine_half] = chosen[...]
    for step in range(1, nband):
        sends[step - 1].wait_recv()
        origin = lax.rem(band + nband - step, nband)
        block = out_ref.at[origin, mine_half]
        relay = remote(block, block, s_rel.at[step], r_rel.at[step], partner)
        relay.start()
        relays.append(relay)
    for relay in relays:
        relay.wait_recv()
    for copy in sends + relays:
        copy.wait_send()
    swap.wait_send()

    @pl.when(z < nz - 1)
    def _():
        rise.wait_send()

    @pl.when(z > 0)
    def _():
        fall.wait_send()


def gather(owner, block, npool, nband):
    half = pltpu.VMEM((TILES // 2, 2, LANES), jnp.float32)
    dma = pltpu.SemaphoreType.DMA
    vmem = pl.BlockSpec(memory_space=pltpu.VMEM)
    return pl.pallas_call(
        functools.partial(gather_kernel, npool, nband),
        out_shape=jax.ShapeDtypeStruct((nband, TILES, 2, LANES), jnp.float32),
        in_specs=[pl.BlockSpec(memory_space=pltpu.SMEM), vmem],
        out_specs=vmem,
        scratch_shapes=[half] * 7 + [dma] * 6 + [dma((nband,))] * 4,
        compiler_params=pltpu.CompilerParams(collective_id=0, has_side_effects=True),
        name="gather",
    )(owner, block)


def shards(npool, nband, orbitals, kpoints, owner):
    block = orbitals.reshape(2, TILES, LANES).transpose(1, 0, 2)
    sources = gather(owner, block, npool, nband)
    total = compute(
        owner, kpoints.T, sources.reshape(nband * 2 * TILES, LANES), block.reshape(2 * TILES, LANES), jnp.asarray(dft_weights())
    )
    return total.reshape(1, 1, 2, GRID)


def solution(mesh):
    placed = (P("pool", "band", None, None), P(), P())
    body = functools.partial(shards, mesh.shape["pool"], mesh.shape["band"])
    return jax.shard_map(
        body, mesh=mesh, in_specs=placed, out_specs=P("pool", "band", None, None), check_vma=False
    )
```

```python
import functools
import math

import jax
import jax.numpy as jnp
import numpy as np
from jax import lax
from jax.experimental import pallas as pl
from jax.experimental.pallas import tpu as pltpu
from jax.sharding import PartitionSpec as P

NG = 24
ROWS = NG * NG
GRID = NG**3
LANES = 128
TILES = GRID // LANES
GROUP = 4

mixing = 0.25
kernel_scale = 60.0
screening = 4.0

MESH = pl.DeviceIdType.MESH


def dft_weights():
    idx = np.arange(NG)
    phase = 2.0 * np.pi * (np.outer(idx, idx) % NG) / NG
    cosine, sine = np.cos(phase), -np.sin(phase)
    full = np.zeros((2 * LANES, 2 * LANES))
    for n in range(GROUP):
        lo = n * NG
        re, im = slice(lo, lo + NG), slice(LANES + lo, LANES + lo + NG)
        full[re, re] = cosine
        full[re, im] = sine
        full[im, re] = -sine
        full[im, im] = cosine
    full = full.astype(np.float32)
    high = full.astype(jnp.bfloat16)
    low = (full - high.astype(np.float32)).astype(jnp.bfloat16)
    return np.stack([high, low])


def cadd(x, y):
    return x[0] + y[0], x[1] + y[1]


def csub(x, y):
    return x[0] - y[0], x[1] - y[1]


def down(x):
    return x[1], -x[0]


def dft3(x0, x1, x2):
    total = cadd(x1, x2)
    diff = csub(x1, x2)
    half = (x0[0] - 0.5 * total[0], x0[1] - 0.5 * total[1])
    root = math.sqrt(3.0) / 2.0
    turn = (root * diff[1], -root * diff[0])
    return cadd(x0, total), cadd(half, turn), csub(half, turn)


def dft4(x0, x1, x2, x3):
    a, b = cadd(x0, x2), csub(x0, x2)
    c, d = cadd(x1, x3), down(csub(x1, x3))
    return cadd(a, c), cadd(b, d), csub(a, c), csub(b, d)


def dft8(x):
    even = dft4(x[0], x[2], x[4], x[6])
    odd = dft4(x[1], x[3], x[5], x[7])
    root = math.sqrt(0.5)
    one, three = odd[1], odd[3]
    twisted = [
        odd[0],
        (root * (one[0] + one[1]), root * (one[1] - one[0])),
        down(odd[2]),
        (root * (three[1] - three[0]), -root * (three[0] + three[1])),
    ]
    return [cadd(even[i], twisted[i]) for i in range(4)] + [csub(even[i], twisted[i]) for i in range(4)]


def dft24(x):
    parts = [[None] * 8 for _ in range(3)]
    for n2 in range(8):
        three = dft3(*(x[(8 * n1 + 3 * n2) % NG] for n1 in range(3)))
        for k1 in range(3):
            parts[k1][n2] = three[k1]
    out = [None] * NG
    for k1 in range(3):
        eight = dft8(parts[k1])
        for k2 in range(8):
            out[next(k for k in range(NG) if k % 3 == k1 and k % 8 == k2)] = eight[k2]
    return out


def lane_iota(shape):
    return lax.broadcasted_iota(jnp.int32, shape, len(shape) - 1)


def starts():
    return [min(8 * i, 28) for i in range(5)]


def compute_kernel(count, owner_ref, kp_ref, src_ref, own_ref, w_ref, out_ref, dre, dim, flat, ker):
    pool = lax.axis_index("pool")
    source = owner_ref[0]
    d0 = kp_ref[0, pool] - kp_ref[0, source]
    d1 = kp_ref[1, pool] - kp_ref[1, source]
    d2 = kp_ref[2, pool] - kp_ref[2, source]
    lane = lane_iota((NG, LANES))
    gc = ((lane % NG + NG // 2) % NG - NG // 2).astype(jnp.float32)
    row = lax.broadcasted_iota(jnp.int32, (NG, LANES), 0)
    gb = ((row + NG // 2) % NG - NG // 2).astype(jnp.float32)
    plane = (gb + d1) ** 2 + (gc + d2) ** 2 + screening
    for a in range(NG):
        ga = float((a + NG // 2) % NG - NG // 2)
        ker[pl.ds(NG * a, NG), :] = (kernel_scale / GRID) / (plane + (ga + d0) ** 2)

    lane8 = lane_iota((8, LANES))
    row8 = lax.broadcasted_iota(jnp.int32, (8, LANES), 0)
    carried = (row8 + 16 + lane8 // NG >= NG) & (lane8 < NG * GROUP)

    def tile(ref, base, start, s, ri):
        if s < 3:
            return ref[pl.ds(base + 6 * start + 2 * s + ri, 8, stride=6), :]
        if start + 8 < 36:
            return ref[pl.ds(base + 6 * (start + 1) + ri, 8, stride=6), :]
        last = pltpu.roll(ref[pl.ds(base + 6 * start + ri, 8, stride=6), :], 7, 0)
        first = ref[pl.ds(base + ri, 8, stride=6), :]
        return jnp.where(row8 == 7, pltpu.roll(first, 7, 0), last)

    def shift(value, amount):
        amount %= LANES
        return pltpu.roll(value, amount, 1) if amount else value

    def line(re_ref, im_ref, first, stride, step, swapped, before=False, after=False):
        def at(i):
            return pl.ds(first + step * i, 8, stride=stride) if stride > 1 else pl.ds(first + step * i, 8)

        def mixed(values, other):
            return [
                tuple(jnp.where(carried, values[(i + other) % NG][c], values[i][c]) for c in range(2)) for i in range(NG)
            ]

        values = [(re_ref[at(i), :], im_ref[at(i), :]) for i in range(NG)]
        if before:
            values = mixed(values, -1)
        if swapped:
            values = [pair[::-1] for pair in values]
        values = dft24(values)
        if swapped:
            values = [pair[::-1] for pair in values]
        if after:
            values = mixed(values, 1)
        for i, pair in enumerate(values):
            re_ref[at(i), :] = pair[0]
            im_ref[at(i), :] = pair[1]

    def product(first, second):
        x = jnp.concatenate([first, second], axis=1)
        high = x.astype(jnp.bfloat16)
        low = (x - high.astype(jnp.float32)).astype(jnp.bfloat16)
        dot = functools.partial(jnp.dot, preferred_element_type=jnp.float32)
        y = dot(high, w_ref[0]) + (dot(low, w_ref[0]) + dot(high, w_ref[1]))
        return y[:, :LANES], y[:, LANES:]

    def convolve(part):
        at = pl.ds(192 * part, 192)
        re, im = product(dre[at, :], dim[at, :])
        value = ker[at, :]
        im, re = product(im * value, re * value)
        dre[at, :] = re
        dim[at, :] = im

    for group in range(count // GROUP):
        bases = [2 * TILES * (group * GROUP + n) for n in range(GROUP)]
        for start in starts():
            density = []
            for s in range(4):
                r_re, r_im = (tile(own_ref, 0, start, s, ri) for ri in range(2))
                cell = []
                for n in range(GROUP):
                    s_re, s_im = (tile(src_ref, bases[n], start, s, ri) for ri in range(2))
                    cell.append((s_re * r_re + s_im * r_im, s_re * r_im - s_im * r_re))
                density.append(cell)
            for j in range(16):
                s, off = divmod(NG * j, LANES)
                for ri, ref in enumerate((dre, dim)):
                    total = None
                    for n in range(GROUP):
                        lo = off + NG * n
                        if lo + NG <= LANES:
                            value = density[s][n][ri]
                        elif lo >= LANES:
                            value = density[s + 1][n][ri]
                        else:
                            value = jnp.where(lane8 >= LANES // 2, density[s][n][ri], density[s + 1][n][ri])
                        if total is None:
                            total = value
                        else:
                            lo, hi = lo % LANES, (lo + NG) % LANES
                            inside = (lane8 >= lo) & (lane8 < hi) if lo < hi else (lane8 >= lo) | (lane8 < hi)
                            total = jnp.where(inside, value, total)
                    ref[pl.ds(16 * start + j, 8, stride=16), :] = shift(total, -off)
        for bg in range(3):
            line(dre, dim, 8 * bg, 1, NG, False, before=bg == 2)
        for ag in range(3):
            line(dre, dim, 8 * NG * ag, NG, 1, False)
        for ag in range(3):
            convolve(ag)
        for ag in range(3):
            line(dre, dim, 8 * NG * ag, NG, 1, True)
        for bg in range(3):
            line(dre, dim, 8 * bg, 1, NG, True, after=bg == 2)
        for start in starts():
            moved = {}
            for j in range(-3, 16):
                for ri, ref in enumerate((dre, dim)):
                    if j >= 0:
                        value = ref[pl.ds(16 * start + j, 8, stride=16), :]
                    elif start:
                        value = ref[pl.ds(16 * (start - 1) + 16 + j, 8, stride=16), :]
                    else:
                        value = pltpu.roll(ref[pl.ds(16 + j, 8, stride=16), :], 1, 0)
                        end = ref[pl.ds(16 * 28 + 16 + j, 8, stride=16), :]
                        value = jnp.where(row8 == 0, pltpu.roll(end, 1, 0), value)
                    moved[j, ri] = shift(value, NG * j)
            for s in range(3):
                first = LANES * s // NG
                last = (LANES * (s + 1) - 1) // NG
                out_re = out_im = None
                for n in range(GROUP):
                    pot = []
                    for ri in range(2):
                        value = moved[first - n, ri]
                        for w in range(first + 1, last + 1):
                            value = jnp.where(lane8 >= NG * w - LANES * s, moved[w - n, ri], value)
                        pot.append(value)
                    s_re, s_im = (tile(src_ref, bases[n], start, s, ri) for ri in range(2))
                    t_re = s_re * pot[0] - s_im * pot[1]
                    t_im = s_re * pot[1] + s_im * pot[0]
                    out_re = t_re if out_re is None else out_re + t_re
                    out_im = t_im if out_im is None else out_im + t_im
                for ri, value in enumerate((out_re, out_im)):
                    at = pl.ds(6 * start + 2 * s + ri, 8, stride=6)
                    value = -mixing * value
                    if group:
                        value = value + flat[group - 1, at, :]
                    flat[group, at, :] = value
    for t in range(TILES):
        out_ref[:, pl.ds(LANES * t, LANES)] = flat[count // GROUP - 1, pl.ds(2 * t, 2), :]


def compute(owner, kpoints, sources, own, weights):
    count = sources.shape[0] // (2 * TILES)
    vmem = pl.BlockSpec(memory_space=pltpu.VMEM)
    smem = pl.BlockSpec(memory_space=pltpu.SMEM)
    return pl.pallas_call(
        functools.partial(compute_kernel, count),
        out_shape=jax.ShapeDtypeStruct((2, GRID), jnp.float32),
        in_specs=[smem, smem, vmem, vmem, vmem],
        out_specs=vmem,
        scratch_shapes=[
            pltpu.VMEM((ROWS, LANES), jnp.float32),
            pltpu.VMEM((ROWS, LANES), jnp.float32),
            pltpu.VMEM((count // GROUP, 2 * TILES, LANES), jnp.float32),
            pltpu.VMEM((ROWS, LANES), jnp.float32),
        ],
        name="exchange",
    )(owner, kpoints, sources, own, weights)


def gather_kernel(npool, nband, pieces, owner_ref, x_ref, out_ref, pair, mine, up, dn, upo, dno,
                  s_pair, r_pair, s_up, r_up, s_dn, r_dn, s_band, r_band, s_rel, r_rel):
    pool, band = lax.axis_index("pool"), lax.axis_index("band")
    nz = npool // 2
    z, core = pool // 2, pool % 2
    half = TILES // 2
    size = half // pieces
    source = owner_ref[0]
    partner = {"pool": 2 * z + 1 - core}
    above = {"pool": lax.rem(pool + 2, npool)}
    below = {"pool": lax.rem(pool + npool - 2, npool)}
    barrier = pltpu.get_barrier_semaphore()
    pl.semaphore_signal(barrier, inc=1, device_id=partner, device_id_type=MESH)
    pl.semaphore_signal(barrier, inc=1, device_id=above, device_id_type=MESH)
    pl.semaphore_signal(barrier, inc=1, device_id=below, device_id_type=MESH)
    for step in range(1, nband):
        pl.semaphore_signal(barrier, inc=1, device_id={"band": lax.rem(band + step, nband)}, device_id_type=MESH)
    pl.semaphore_wait(barrier, 3 + nband - 1)

    def remote(src, dst, ss, rs, to):
        return pltpu.make_async_remote_copy(src_ref=src, dst_ref=dst, send_sem=ss, recv_sem=rs, device_id=to, device_id_type=MESH)

    def cut(k):
        return pl.ds(size * k, size)

    swaps = [
        remote(x_ref.at[pl.ds(half * (1 - core) + size * k, size)], pair.at[cut(k)], s_pair.at[k], r_pair.at[k], partner)
        for k in range(pieces)
    ]
    rises = [remote(upo.at[cut(k)], up.at[cut(k)], s_up.at[k], r_up.at[k], above) for k in range(pieces)]
    falls = [remote(dno.at[cut(k)], dn.at[cut(k)], s_dn.at[k], r_dn.at[k], below) for k in range(pieces)]
    spreads = [[None] * nband for _ in range(pieces)]
    relays = [[None] * nband for _ in range(pieces)]
    for k in range(pieces):
        block_at = pl.ds(half * core + size * k, size)
        for step in range(nband):
            block = out_ref.at[lax.rem(band + nband - step, nband), block_at]
            relays[k][step] = remote(block, block, s_rel.at[k, step], r_rel.at[k, step], partner)
            if step:
                block = out_ref.at[band, block_at]
                spreads[k][step] = remote(
                    block, block, s_band.at[k, step], r_band.at[k, step], {"band": lax.rem(band + step, nband)}
                )
    for swap in swaps:
        swap.start()

    def take(k):
        swaps[k].wait_recv()
        keep = x_ref[pl.ds(half * core + size * k, size)]
        got = pair[cut(k)]
        other = jnp.where(source == 2 * z + 1 - core, got, jnp.zeros_like(got))
        mine[cut(k)] = jnp.where(source == pool, keep, other)

    def finish(k):
        total = mine[cut(k)]
        out_ref[band, pl.ds(half * core + size * k, size)] = total + up[cut(k)] + dn[cut(k)]
        for step in range(1, nband):
            spreads[k][step].start()
        relays[k][0].start()

    def run(near, near_out, nears, far, far_out, fars, at_near_end, at_far_end):
        @pl.when(at_near_end)
        def _():
            near[...] = jnp.zeros_like(near)
            for k in range(pieces):
                take(k)
                near_out[cut(k)] = mine[cut(k)]
                nears[k].start()

        @pl.when(jnp.logical_not(at_near_end))
        def _():
            for k in range(pieces):
                take(k)
            for k in range(pieces):
                nears[k].wait_recv()

                @pl.when(jnp.logical_not(at_far_end))
                def _():
                    near_out[cut(k)] = near[cut(k)] + mine[cut(k)]
                    nears[k].start()

        @pl.when(at_far_end)
        def _():
            far[...] = jnp.zeros_like(far)

        for k in range(pieces):
            @pl.when(jnp.logical_not(at_far_end))
            def _():
                fars[k].wait_recv()

            @pl.when(jnp.logical_not(at_near_end))
            def _():
                far_out[cut(k)] = far[cut(k)] + mine[cut(k)]
                fars[k].start()

            finish(k)

    bottom, top = z == 0, z == nz - 1

    @pl.when(z < nz // 2)
    def _():
        run(up, upo, rises, dn, dno, falls, bottom, top)

    @pl.when(z >= nz // 2)
    def _():
        if nz > 1:
            run(dn, dno, falls, up, upo, rises, top, bottom)

    for k in range(pieces):
        for step in range(1, nband):
            spreads[k][step].wait_recv()
            relays[k][step].start()
    for k in range(pieces):
        for step in range(nband):
            relays[k][step].wait_recv()
    for k in range(pieces):
        swaps[k].wait_send()
        for step in range(nband):
            relays[k][step].wait_send()
            if step:
                spreads[k][step].wait_send()

        @pl.when(jnp.logical_not(top))
        def _():
            rises[k].wait_send()

        @pl.when(jnp.logical_not(bottom))
        def _():
            falls[k].wait_send()


def gather(owner, block, npool, nband, pieces=3):
    half = pltpu.VMEM((TILES // 2, 2, LANES), jnp.float32)
    dma = pltpu.SemaphoreType.DMA
    vmem = pl.BlockSpec(memory_space=pltpu.VMEM)
    return pl.pallas_call(
        functools.partial(gather_kernel, npool, nband, pieces),
        out_shape=pltpu.VMEM((nband, TILES, 2, LANES), jnp.float32),
        in_specs=[pl.BlockSpec(memory_space=pltpu.SMEM), vmem],
        out_specs=vmem,
        scratch_shapes=[half] * 6 + [dma((pieces,))] * 6 + [dma((pieces, nband))] * 4,
        compiler_params=pltpu.CompilerParams(collective_id=0, has_side_effects=True),
        name="gather",
    )(owner, block)


def shards(npool, nband, orbitals, kpoints, owner):
    block = orbitals.reshape(2, TILES, LANES).transpose(1, 0, 2)
    sources = gather(owner, block, npool, nband)
    total = compute(
        owner, kpoints.T, pltpu.with_memory_space_constraint(sources.reshape(nband * 2 * TILES, LANES), pltpu.VMEM), block.reshape(2 * TILES, LANES), jnp.asarray(dft_weights())
    )
    return total.reshape(1, 1, 2, GRID)


def solution(mesh):
    placed = (P("pool", "band", None, None), P(), P())
    body = functools.partial(shards, mesh.shape["pool"], mesh.shape["band"])
    return jax.shard_map(
        body, mesh=mesh, in_specs=placed, out_specs=P("pool", "band", None, None), check_vma=False
    )
```

```python
import functools
import math

import jax
import jax.numpy as jnp
import numpy as np
from jax import lax
from jax.experimental import pallas as pl
from jax.experimental.pallas import tpu as pltpu
from jax.sharding import PartitionSpec as P

NG = 24
ROWS = NG * NG
GRID = NG**3
LANES = 128
TILES = GRID // LANES
GROUP = 4

mixing = 0.25
kernel_scale = 60.0
screening = 4.0

MESH = pl.DeviceIdType.MESH


def dft_weights():
    idx = np.arange(NG)
    phase = 2.0 * np.pi * (np.outer(idx, idx) % NG) / NG
    cosine, sine = np.cos(phase), -np.sin(phase)
    full = np.zeros((2 * LANES, 2 * LANES))
    for n in range(GROUP):
        lo = n * NG
        re, im = slice(lo, lo + NG), slice(LANES + lo, LANES + lo + NG)
        full[re, re] = cosine
        full[re, im] = sine
        full[im, re] = -sine
        full[im, im] = cosine
    full = full.astype(np.float32)
    high = full.astype(jnp.bfloat16)
    low = (full - high.astype(np.float32)).astype(jnp.bfloat16)
    return np.stack([high, low])


def cadd(x, y):
    return x[0] + y[0], x[1] + y[1]


def csub(x, y):
    return x[0] - y[0], x[1] - y[1]


def down(x):
    return x[1], -x[0]


def dft3(x0, x1, x2):
    total = cadd(x1, x2)
    diff = csub(x1, x2)
    half = (x0[0] - 0.5 * total[0], x0[1] - 0.5 * total[1])
    root = math.sqrt(3.0) / 2.0
    turn = (root * diff[1], -root * diff[0])
    return cadd(x0, total), cadd(half, turn), csub(half, turn)


def dft4(x0, x1, x2, x3):
    a, b = cadd(x0, x2), csub(x0, x2)
    c, d = cadd(x1, x3), down(csub(x1, x3))
    return cadd(a, c), cadd(b, d), csub(a, c), csub(b, d)


def dft8(x):
    even = dft4(x[0], x[2], x[4], x[6])
    odd = dft4(x[1], x[3], x[5], x[7])
    root = math.sqrt(0.5)
    one, three = odd[1], odd[3]
    twisted = [
        odd[0],
        (root * (one[0] + one[1]), root * (one[1] - one[0])),
        down(odd[2]),
        (root * (three[1] - three[0]), -root * (three[0] + three[1])),
    ]
    return [cadd(even[i], twisted[i]) for i in range(4)] + [csub(even[i], twisted[i]) for i in range(4)]


def dft24(x):
    parts = [[None] * 8 for _ in range(3)]
    for n2 in range(8):
        three = dft3(*(x[(8 * n1 + 3 * n2) % NG] for n1 in range(3)))
        for k1 in range(3):
            parts[k1][n2] = three[k1]
    out = [None] * NG
    for k1 in range(3):
        eight = dft8(parts[k1])
        for k2 in range(8):
            out[next(k for k in range(NG) if k % 3 == k1 and k % 8 == k2)] = eight[k2]
    return out


def lane_iota(shape):
    return lax.broadcasted_iota(jnp.int32, shape, len(shape) - 1)


def starts():
    return [min(8 * i, 28) for i in range(5)]


def compute_kernel(count, owner_ref, kp_ref, src_ref, own_ref, w_ref, out_ref, dre, dim, flat, ker):
    pool = lax.axis_index("pool")
    source = owner_ref[0]
    d0 = kp_ref[0, pool] - kp_ref[0, source]
    d1 = kp_ref[1, pool] - kp_ref[1, source]
    d2 = kp_ref[2, pool] - kp_ref[2, source]
    lane = lane_iota((NG, LANES))
    gc = ((lane % NG + NG // 2) % NG - NG // 2).astype(jnp.float32)
    row = lax.broadcasted_iota(jnp.int32, (NG, LANES), 0)
    gb = ((row + NG // 2) % NG - NG // 2).astype(jnp.float32)
    plane = (gb + d1) ** 2 + (gc + d2) ** 2 + screening
    for a in range(NG):
        ga = float((a + NG // 2) % NG - NG // 2)
        ker[pl.ds(NG * a, NG), :] = (kernel_scale / GRID) / (plane + (ga + d0) ** 2)

    lane8 = lane_iota((8, LANES))
    row8 = lax.broadcasted_iota(jnp.int32, (8, LANES), 0)
    carried = (row8 + 16 + lane8 // NG >= NG) & (lane8 < NG * GROUP)

    def tile(ref, base, start, s, ri):
        if s < 3:
            return ref[pl.ds(base + 6 * start + 2 * s + ri, 8, stride=6), :]
        if start + 8 < 36:
            return ref[pl.ds(base + 6 * (start + 1) + ri, 8, stride=6), :]
        last = pltpu.roll(ref[pl.ds(base + 6 * start + ri, 8, stride=6), :], 7, 0)
        first = ref[pl.ds(base + ri, 8, stride=6), :]
        return jnp.where(row8 == 7, pltpu.roll(first, 7, 0), last)

    def shift(value, amount):
        amount %= LANES
        return pltpu.roll(value, amount, 1) if amount else value

    def line(re_ref, im_ref, first, stride, step, swapped, before=False, after=False):
        def at(i):
            return pl.ds(first + step * i, 8, stride=stride) if stride > 1 else pl.ds(first + step * i, 8)

        def mixed(values, other):
            return [
                tuple(jnp.where(carried, values[(i + other) % NG][c], values[i][c]) for c in range(2)) for i in range(NG)
            ]

        values = [(re_ref[at(i), :], im_ref[at(i), :]) for i in range(NG)]
        if before:
            values = mixed(values, -1)
        if swapped:
            values = [pair[::-1] for pair in values]
        values = dft24(values)
        if swapped:
            values = [pair[::-1] for pair in values]
        if after:
            values = mixed(values, 1)
        for i, pair in enumerate(values):
            re_ref[at(i), :] = pair[0]
            im_ref[at(i), :] = pair[1]

    def product(first, second):
        x = jnp.concatenate([first, second], axis=1)
        high = x.astype(jnp.bfloat16)
        low = (x - high.astype(jnp.float32)).astype(jnp.bfloat16)
        dot = functools.partial(jnp.dot, preferred_element_type=jnp.float32)
        y = dot(high, w_ref[0]) + (dot(low, w_ref[0]) + dot(high, w_ref[1]))
        return y[:, :LANES], y[:, LANES:]

    def convolve(part):
        at = pl.ds(192 * part, 192)
        re, im = product(dre[at, :], dim[at, :])
        value = ker[at, :]
        im, re = product(im * value, re * value)
        dre[at, :] = re
        dim[at, :] = im

    for group in range(count // GROUP):
        bases = [2 * TILES * (group * GROUP + n) for n in range(GROUP)]
        for start in starts():
            density = []
            for s in range(4):
                r_re, r_im = (tile(own_ref, 0, start, s, ri) for ri in range(2))
                cell = []
                for n in range(GROUP):
                    s_re, s_im = (tile(src_ref, bases[n], start, s, ri) for ri in range(2))
                    cell.append((s_re * r_re + s_im * r_im, s_re * r_im - s_im * r_re))
                density.append(cell)
            for j in range(16):
                s, off = divmod(NG * j, LANES)
                for ri, ref in enumerate((dre, dim)):
                    total = None
                    for n in range(GROUP):
                        lo = off + NG * n
                        if lo + NG <= LANES:
                            value = density[s][n][ri]
                        elif lo >= LANES:
                            value = density[s + 1][n][ri]
                        else:
                            value = jnp.where(lane8 >= LANES // 2, density[s][n][ri], density[s + 1][n][ri])
                        if total is None:
                            total = value
                        else:
                            lo, hi = lo % LANES, (lo + NG) % LANES
                            inside = (lane8 >= lo) & (lane8 < hi) if lo < hi else (lane8 >= lo) | (lane8 < hi)
                            total = jnp.where(inside, value, total)
                    ref[pl.ds(16 * start + j, 8, stride=16), :] = shift(total, -off)
        for bg in range(3):
            line(dre, dim, 8 * bg, 1, NG, False, before=bg == 2)
        for ag in range(3):
            line(dre, dim, 8 * NG * ag, NG, 1, False)
        for ag in range(3):
            convolve(ag)
        for ag in range(3):
            line(dre, dim, 8 * NG * ag, NG, 1, True)
        for bg in range(3):
            line(dre, dim, 8 * bg, 1, NG, True, after=bg == 2)
        for start in starts():
            moved = {}
            for j in range(-3, 16):
                for ri, ref in enumerate((dre, dim)):
                    if j >= 0:
                        value = ref[pl.ds(16 * start + j, 8, stride=16), :]
                    elif start:
                        value = ref[pl.ds(16 * (start - 1) + 16 + j, 8, stride=16), :]
                    else:
                        value = pltpu.roll(ref[pl.ds(16 + j, 8, stride=16), :], 1, 0)
                        end = ref[pl.ds(16 * 28 + 16 + j, 8, stride=16), :]
                        value = jnp.where(row8 == 0, pltpu.roll(end, 1, 0), value)
                    moved[j, ri] = shift(value, NG * j)
            for s in range(3):
                first = LANES * s // NG
                last = (LANES * (s + 1) - 1) // NG
                out_re = out_im = None
                for n in range(GROUP):
                    pot = []
                    for ri in range(2):
                        value = moved[first - n, ri]
                        for w in range(first + 1, last + 1):
                            value = jnp.where(lane8 >= NG * w - LANES * s, moved[w - n, ri], value)
                        pot.append(value)
                    s_re, s_im = (tile(src_ref, bases[n], start, s, ri) for ri in range(2))
                    t_re = s_re * pot[0] - s_im * pot[1]
                    t_im = s_re * pot[1] + s_im * pot[0]
                    out_re = t_re if out_re is None else out_re + t_re
                    out_im = t_im if out_im is None else out_im + t_im
                for ri, value in enumerate((out_re, out_im)):
                    at = pl.ds(6 * start + 2 * s + ri, 8, stride=6)
                    value = -mixing * value
                    if group:
                        value = value + flat[group - 1, at, :]
                    flat[group, at, :] = value
    for t in range(TILES):
        out_ref[:, pl.ds(LANES * t, LANES)] = flat[count // GROUP - 1, pl.ds(2 * t, 2), :]


def compute(owner, kpoints, sources, own, weights):
    count = sources.shape[0] // (2 * TILES)
    vmem = pl.BlockSpec(memory_space=pltpu.VMEM)
    smem = pl.BlockSpec(memory_space=pltpu.SMEM)
    return pl.pallas_call(
        functools.partial(compute_kernel, count),
        out_shape=jax.ShapeDtypeStruct((2, GRID), jnp.float32),
        in_specs=[smem, smem, vmem, vmem, vmem],
        out_specs=vmem,
        scratch_shapes=[
            pltpu.VMEM((ROWS, LANES), jnp.float32),
            pltpu.VMEM((ROWS, LANES), jnp.float32),
            pltpu.VMEM((count // GROUP, 2 * TILES, LANES), jnp.float32),
            pltpu.VMEM((ROWS, LANES), jnp.float32),
        ],
        name="exchange",
    )(owner, kpoints, sources, own, weights)


def gather_kernel(npool, nband, pieces, owner_ref, x_ref, out_ref, pair, mine, up, dn, upo, dno,
                  s_pair, r_pair, s_up, r_up, s_dn, r_dn, s_band, r_band, s_rel, r_rel):
    pool, band = lax.axis_index("pool"), lax.axis_index("band")
    nz = npool // 2
    z, core = pool // 2, pool % 2
    half = TILES // 2
    size = half // pieces
    source = owner_ref[0]
    partner = {"pool": 2 * z + 1 - core}
    above = {"pool": lax.rem(pool + 2, npool)}
    below = {"pool": lax.rem(pool + npool - 2, npool)}
    barrier = pltpu.get_barrier_semaphore()
    pl.semaphore_signal(barrier, inc=1, device_id=partner, device_id_type=MESH)
    pl.semaphore_signal(barrier, inc=1, device_id=above, device_id_type=MESH)
    pl.semaphore_signal(barrier, inc=1, device_id=below, device_id_type=MESH)
    for step in range(1, nband):
        pl.semaphore_signal(barrier, inc=1, device_id={"band": lax.rem(band + step, nband)}, device_id_type=MESH)
    pl.semaphore_wait(barrier, 3 + nband - 1)

    def remote(src, dst, ss, rs, to):
        return pltpu.make_async_remote_copy(src_ref=src, dst_ref=dst, send_sem=ss, recv_sem=rs, device_id=to, device_id_type=MESH)

    def cut(k):
        return pl.ds(size * k, size)

    swaps = [
        remote(x_ref.at[pl.ds(half * (1 - core) + size * k, size)], pair.at[cut(k)], s_pair.at[k], r_pair.at[k], partner)
        for k in range(pieces)
    ]
    rises = [remote(upo.at[cut(k)], up.at[cut(k)], s_up.at[k], r_up.at[k], above) for k in range(pieces)]
    falls = [remote(dno.at[cut(k)], dn.at[cut(k)], s_dn.at[k], r_dn.at[k], below) for k in range(pieces)]
    spreads = [[None] * nband for _ in range(pieces)]
    relays = [[None] * nband for _ in range(pieces)]
    for k in range(pieces):
        block_at = pl.ds(half * core + size * k, size)
        for step in range(nband):
            block = out_ref.at[lax.rem(band + nband - step, nband), block_at]
            relays[k][step] = remote(block, block, s_rel.at[k, step], r_rel.at[k, step], partner)
            if step:
                block = out_ref.at[band, block_at]
                spreads[k][step] = remote(
                    block, block, s_band.at[k, step], r_band.at[k, step], {"band": lax.rem(band + step, nband)}
                )
    for swap in swaps:
        swap.start()

    def take(k):
        swaps[k].wait_recv()
        keep = x_ref[pl.ds(half * core + size * k, size)]
        got = pair[cut(k)]
        other = jnp.where(source == 2 * z + 1 - core, got, jnp.zeros_like(got))
        mine[cut(k)] = jnp.where(source == pool, keep, other)

    def finish(k):
        total = mine[cut(k)]
        out_ref[band, pl.ds(half * core + size * k, size)] = total + up[cut(k)] + dn[cut(k)]
        for step in range(1, nband):
            spreads[k][step].start()
        relays[k][0].start()

    def run(near, near_out, nears, far, far_out, fars, at_near_end, at_far_end):
        @pl.when(at_near_end)
        def _():
            near[...] = jnp.zeros_like(near)
            for k in range(pieces):
                take(k)
                near_out[cut(k)] = mine[cut(k)]
                nears[k].start()

        @pl.when(jnp.logical_not(at_near_end))
        def _():
            for k in range(pieces):
                take(k)
            for k in range(pieces):
                nears[k].wait_recv()

                @pl.when(jnp.logical_not(at_far_end))
                def _():
                    near_out[cut(k)] = near[cut(k)] + mine[cut(k)]
                    nears[k].start()

        @pl.when(at_far_end)
        def _():
            far[...] = jnp.zeros_like(far)

        for k in range(pieces):
            @pl.when(jnp.logical_not(at_far_end))
            def _():
                fars[k].wait_recv()

            @pl.when(jnp.logical_not(at_near_end))
            def _():
                far_out[cut(k)] = far[cut(k)] + mine[cut(k)]
                fars[k].start()

            finish(k)

    bottom, top = z == 0, z == nz - 1

    @pl.when(z < nz // 2)
    def _():
        run(up, upo, rises, dn, dno, falls, bottom, top)

    @pl.when(z >= nz // 2)
    def _():
        if nz > 1:
            run(dn, dno, falls, up, upo, rises, top, bottom)

    for k in range(pieces):
        for step in range(1, nband):
            spreads[k][step].wait_recv()
            relays[k][step].start()
    for k in range(pieces):
        for step in range(nband):
            relays[k][step].wait_recv()
    for k in range(pieces):
        swaps[k].wait_send()
        for step in range(nband):
            relays[k][step].wait_send()
            if step:
                spreads[k][step].wait_send()

        @pl.when(jnp.logical_not(top))
        def _():
            rises[k].wait_send()

        @pl.when(jnp.logical_not(bottom))
        def _():
            falls[k].wait_send()


def gather(owner, block, npool, nband, pieces=3):
    half = pltpu.VMEM((TILES // 2, 2, LANES), jnp.float32)
    dma = pltpu.SemaphoreType.DMA
    vmem = pl.BlockSpec(memory_space=pltpu.VMEM)
    return pl.pallas_call(
        functools.partial(gather_kernel, npool, nband, pieces),
        out_shape=pltpu.VMEM((nband, TILES, 2, LANES), jnp.float32),
        in_specs=[pl.BlockSpec(memory_space=pltpu.SMEM), vmem],
        out_specs=vmem,
        scratch_shapes=[half] * 6 + [dma((pieces,))] * 6 + [dma((pieces, nband))] * 4,
        compiler_params=pltpu.CompilerParams(collective_id=0, has_side_effects=True),
        name="gather",
    )(owner, block)


def shards(npool, nband, orbitals, kpoints, owner):
    block = orbitals.reshape(2, TILES, LANES).transpose(1, 0, 2)
    sources = gather(owner, block, npool, nband)
    near = functools.partial(pltpu.with_memory_space_constraint, memory_space=pltpu.VMEM)
    total = compute(
        owner,
        kpoints.T,
        near(sources.reshape(nband * 2 * TILES, LANES)),
        near(block.reshape(2 * TILES, LANES)),
        near(jnp.asarray(dft_weights())),
    )
    return total.reshape(1, 1, 2, GRID)


def solution(mesh):
    placed = (P("pool", "band", None, None), P(), P())
    body = functools.partial(shards, mesh.shape["pool"], mesh.shape["band"])
    return jax.shard_map(
        body, mesh=mesh, in_specs=placed, out_specs=P("pool", "band", None, None), check_vma=False
    )
```
